512 devices in a mesh: section: 4 (over y_lo, core), dp: 4 (over y_hi), expert: 32 (over z, x).
Axes of the slice: x: 4, y: 8 (y_hi: 4, y_lo: 2; y = y_hi * 2 + y_lo), z: 8, core: 2. Of those that a mesh axis runs over, the one named last changes fastest.
Arguments:
- stream: bfloat16 [4, 16384, 2048], P('section', ('dp', 'expert')), may hold values from -60 to 60
- norm_gain: bfloat16 [4, 2048], P('section'), may hold values from 0.29882812 to 3
- gate_probs: float32 [4, 16384, 8], P('section', ('dp', 'expert')), may hold values from 0.02 to 1
- expert_ids: int32 [4, 16384, 8], P('section', ('dp', 'expert')), may hold values from 0 to 127, as said below
- gate_up_weight: bfloat16 [4, 32, 2, 2048, 1024], P('section', 'expert', None, None, 'dp'), may hold values from -0.125 to 0.125
- down_weight: bfloat16 [4, 32, 1024, 2048], P('section', 'expert', 'dp'), may hold values from -0.1875 to 0.1875
Outputs:
- handed: bfloat16 [4, 16384, 2048], P('section', ('dp', 'expert'))
The draws below stay inside these ranges and needn't reach their ends.
Inputs may be any that keep to these rules, and one draw needn't show every extreme that they name: `expert_ids`: each row names 8 different experts. In the rows of one device each expert below 32 is named by at most 12 rows; in each section one such expert is named by exactly 12 rows in the rows of every device.
All inputs are finite; a program needn't handle non-finite values.
Results may differ from the reference program's by a relative error of at most 0.0077.
Values may be sent and summed in bfloat16 or wider, within the bound.
A program may use at most 128 MiB of HBM per device.

```python
import math
import jax
import jax.numpy as jnp
from jax import lax

D = 2048
FFW = 1024
EXPERTS_ALL = 128
TOPK = 8
TOK_DEV = 128
HELD = 32
CAP = 12
TOKENS = 16384
N_SECTION = 4
N_DP = 4


def draw_stream(key, part):
    row_key, column_key, base_key = jax.random.split(key, 3)
    row_scales = jnp.exp(jax.random.uniform(row_key, (N_SECTION, TOKENS, 1), jnp.float32, jnp.log(0.3), jnp.log(3.0)))
    column_scales = jnp.exp(jax.random.uniform(column_key, (N_SECTION, 1, D), jnp.float32, jnp.log(0.5), jnp.log(5.0)))
    base_draw = jnp.clip(jax.random.normal(base_key, (N_SECTION, TOKENS, D), jnp.float32), -4.0, 4.0)
    widened = base_draw * row_scales * column_scales
    return widened.astype(jnp.bfloat16)


def draw_expert_ids(key, part):
    per_section = TOKENS // TOK_DEV
    block_count = N_SECTION * per_section
    others = EXPERTS_ALL - HELD
    slot_total = TOK_DEV * TOPK
    hot_key, low_key, spread_key, order_key, row_key = jax.random.split(key, 5)
    hottest = jax.random.randint(hot_key, (N_SECTION,), 0, HELD)
    hot_block = jnp.repeat(hottest, per_section)
    held_load = jax.random.randint(low_key, (block_count, HELD), 0, CAP + 1)
    held_load = jnp.where(jnp.arange(HELD)[None, :] == hot_block[:, None], CAP, held_load)
    remaining = slot_total - jnp.sum(held_load, axis=1)
    spread_keys = jax.random.split(spread_key, block_count)
    ranking = jax.vmap(lambda subkey: jax.random.permutation(subkey, others))(spread_keys)
    other_load = (remaining // others)[:, None] + (ranking < (remaining % others)[:, None]).astype(jnp.int32)
    loads = jnp.concatenate([held_load, other_load], axis=1)
    order_keys = jax.random.split(order_key, block_count)
    listing = jax.vmap(lambda subkey: jax.random.permutation(subkey, EXPERTS_ALL))(order_keys)
    listed_loads = jnp.take_along_axis(loads, listing, axis=1)
    bounds = jnp.cumsum(listed_loads, axis=1)
    spots = jnp.arange(slot_total, dtype=jnp.int32)
    located = jax.vmap(lambda bound_row: jnp.searchsorted(bound_row, spots, side='right'))(bounds)
    named = jnp.take_along_axis(listing, located, axis=1)
    row_keys = jax.random.split(row_key, block_count)
    row_order = jax.vmap(lambda subkey: jax.random.permutation(subkey, TOK_DEV))(row_keys)
    picks = row_order[:, :, None] + TOK_DEV * jnp.arange(TOPK, dtype=jnp.int32)[None, None, :]
    chosen = jnp.take_along_axis(named, picks.reshape(block_count, TOK_DEV * TOPK), axis=1)
    return chosen.reshape(N_SECTION, TOKENS, TOPK).astype(jnp.int32)


def levels(stream_key, dims, cuts, smallest, top_value):
    def one(dim, blocks):
        steps = jax.random.uniform(jax.random.fold_in(jax.random.fold_in(stream_key, 6), dim), (blocks,), jnp.float32, smallest / len(cuts), top_value / len(cuts))
        return jnp.repeat(jnp.exp(steps), dims[dim] // blocks).reshape((-1,) + (1,) * (len(dims) - dim - 1))

    gain = one(*cuts[0])
    for cut in cuts[1:]:
        gain = gain * one(*cut)
    return gain


def scatter_about(key, dims, spread, reach, pieces=(), kind=jnp.bfloat16):
    gain = levels(key, dims, pieces, -0.22, 0.18) if pieces else 1.0
    entries = jax.random.normal(key, dims, jnp.float32) * spread * gain
    return jnp.minimum(jnp.maximum(entries, -reach), reach).astype(kind)


def setup_inputs(seed: int = 0) -> dict:
    splits = jax.random.split(jax.random.key(seed), 7)
    return {
        "stream": draw_stream(jax.random.fold_in(splits[6], 71), 0),
        "norm_gain": jnp.clip(jnp.exp(math.log(3.0) - 2.306499 * jax.random.uniform(splits[1], (N_SECTION, D), jnp.float32) ** levels(splits[1], (N_SECTION, D), ((0, 4),), -0.2, 0.2)), 0.29882812, 3.0).astype(jnp.bfloat16),
        "gate_probs": jnp.clip(jnp.exp(math.log(1.0) - 3.912023 * jax.random.uniform(splits[2], (N_SECTION, TOKENS, TOPK), jnp.float32) ** levels(splits[2], (N_SECTION, TOKENS, TOPK), ((0, 4), (1, 128)), -0.2, 0.2)), 0.02, 1.0),
        "expert_ids": draw_expert_ids(jax.random.fold_in(splits[6], 71), 0),
        "gate_up_weight": scatter_about(splits[4], (N_SECTION, HELD, 2, D, FFW), D ** -0.5, 0.125, ((0, 4), (1, 32), (4, 4))),
        "down_weight": scatter_about(splits[5], (N_SECTION, HELD, FFW, D), FFW ** -0.5, 0.1875, ((0, 4), (1, 32), (2, 4))),
    }


epsilon = 1e-06

def normalize(activations, gain_row):
    widened = activations.astype(jnp.float32)
    inverse_rms = lax.rsqrt(lax.optimization_barrier(jnp.mean(widened * widened, axis=-1, keepdims=True)) + epsilon)
    return (widened * inverse_rms * gain_row.astype(jnp.float32)).astype(jnp.bfloat16)

def slot_tables(gate_probs, expert_ids, held_count, capacity):
    weights = gate_probs / lax.optimization_barrier(jnp.sum(gate_probs, axis=-1, keepdims=True))
    experts = jnp.arange(held_count, dtype=jnp.int32)
    matches = expert_ids[..., None] == experts
    coefficient = lax.optimization_barrier(jnp.sum(jnp.where(matches, weights[..., None], jnp.float32(0.0)), axis=-2))
    chosen = jnp.any(matches, axis=-2).astype(jnp.int32)
    position = jnp.cumsum(chosen, axis=-2) - chosen
    places = jnp.arange(capacity, dtype=jnp.int32)
    slot_table = (chosen[..., None] == 1) & (position[..., None] == places)
    return (coefficient, slot_table)

def expert_quarter(slot_rows, gate_matrix, up_matrix, down_matrix):
    gate_rows = jnp.dot(slot_rows, gate_matrix, preferred_element_type=jnp.float32)
    up_rows = jnp.dot(slot_rows, up_matrix, preferred_element_type=jnp.float32)
    hidden = (jax.nn.silu(gate_rows) * up_rows).astype(jnp.bfloat16)
    return jnp.dot(hidden, down_matrix, preferred_element_type=jnp.float32).astype(jnp.bfloat16)

def reference(stream, norm_gain, gate_probs, expert_ids, gate_up_weight, down_weight):
    block_count = TOKENS // TOK_DEV
    quarter = FFW // N_DP
    results = []
    for section_index in range(N_SECTION):
        normed = normalize(stream[section_index], norm_gain[section_index]).reshape(block_count, TOK_DEV, D)
        coefficient, slot_table = slot_tables(gate_probs[section_index].reshape(block_count, TOK_DEV, TOPK), expert_ids[section_index].reshape(block_count, TOK_DEV, TOPK), HELD, CAP)
        slot_onehot = slot_table.astype(jnp.float32)
        normed_wide = normed.astype(jnp.float32)
        section_gate_up = gate_up_weight[section_index]
        section_down = down_weight[section_index]

        def add_expert(expert, mixture):
            picked = lax.dynamic_index_in_dim(slot_onehot, expert, 2, keepdims=False)
            slot_rows = jnp.einsum('btc,btd->bcd', picked, normed_wide, precision=lax.Precision.HIGHEST).astype(jnp.bfloat16)
            slot_rows = slot_rows.reshape(block_count * CAP, D)
            weights_in = lax.dynamic_index_in_dim(section_gate_up, expert, 0, keepdims=False)
            weights_out = lax.dynamic_index_in_dim(section_down, expert, 0, keepdims=False)
            summed = jnp.zeros((block_count * CAP, D), jnp.float32)
            for part_index in range(N_DP):
                first = part_index * quarter
                partial_rows = expert_quarter(slot_rows, weights_in[0, :, first:first + quarter], weights_in[1, :, first:first + quarter], weights_out[first:first + quarter, :])
                summed = summed + partial_rows.astype(jnp.float32)
            rounded = lax.optimization_barrier(summed.astype(jnp.bfloat16)).astype(jnp.float32)
            shares = picked * lax.dynamic_index_in_dim(coefficient, expert, 2, keepdims=False)[..., None]
            return mixture + jnp.einsum('btc,bcd->btd', shares, rounded.reshape(block_count, CAP, D), precision=lax.Precision.HIGHEST)
        mixture = lax.fori_loop(0, HELD, add_expert, jnp.zeros((block_count, TOK_DEV, D), jnp.float32))
        results.append(mixture.reshape(TOKENS, D).astype(jnp.bfloat16))
    branches = jnp.stack(results)
    return jnp.roll(branches, 1, axis=0)
```

```python
import jax
import jax.numpy as jnp
from jax import lax
from jax.sharding import PartitionSpec as P

CAP = 12


epsilon = 1e-06


def from_behind(value, axis, steps):
    count = lax.axis_size(axis)
    pairs = [(source, (source + steps) % count) for source in range(count)]
    return lax.ppermute(value, axis, pairs)


def along_dp(value, weights):
    sections = lax.axis_size("section")
    groups = lax.axis_size("dp")
    pairs = []
    for section in range(sections):
        for group in range(groups):
            near = (section % 2 == 0) == weights
            other = group ^ 1 if near else groups - 1 - group
            pairs.append((section * groups + group, section * groups + other))
    return lax.ppermute(value, ("section", "dp"), pairs)


def normalize(activations, gain_row):
    widened = activations.astype(jnp.float32)
    inverse_rms = lax.rsqrt(jnp.mean(widened * widened, axis=-1, keepdims=True) + epsilon)
    return (widened * inverse_rms * gain_row.astype(jnp.float32)).astype(jnp.bfloat16)


def slot_tables(expert_ids, held_count, capacity):
    experts = jnp.arange(held_count, dtype=jnp.int32)
    matches = expert_ids[..., None] == experts
    chosen = jnp.any(matches, axis=-2).astype(jnp.int32)
    position = jnp.cumsum(chosen, axis=-2) - chosen
    places = jnp.arange(capacity, dtype=jnp.int32)
    return matches, (chosen[..., None] == 1) & (position[..., None] == places)


def hidden_quarter(rows, gate_up):
    gate_rows = jnp.dot(rows, gate_up[0], preferred_element_type=jnp.float32)
    up_rows = jnp.dot(rows, gate_up[1], preferred_element_type=jnp.float32)
    return (jax.nn.silu(gate_rows) * up_rows).astype(jnp.bfloat16)


def shards(stream, norm_gain, gate_probs, expert_ids, gate_up_weight, down_weight):
    held_count = lax.axis_size("expert")
    gate_up = gate_up_weight[0, 0]
    down_matrix = down_weight[0, 0]
    ids = expert_ids[0]
    normed = normalize(stream[0], norm_gain[0])
    other_normed = along_dp(normed, False)
    other_ids = along_dp(ids, False)
    other_gate_up = along_dp(gate_up, True)
    other_down = along_dp(down_matrix, True)
    matches, slot_table = slot_tables(ids, held_count, CAP)
    _, other_table = slot_tables(other_ids, held_count, CAP)
    weights = gate_probs[0] / jnp.sum(gate_probs[0], axis=-1, keepdims=True)
    coefficient = jnp.sum(jnp.where(matches, weights[..., None], jnp.float32(0.0)), axis=-2)
    feature_count = normed.shape[1]
    packed = jnp.einsum(
        "dtec,dtf->edcf",
        jnp.stack([slot_table, other_table]).astype(jnp.bfloat16),
        jnp.stack([normed, other_normed]),
        preferred_element_type=jnp.float32,
    ).astype(jnp.bfloat16)
    packed = packed.reshape(held_count, 2 * CAP, feature_count)
    received = lax.all_to_all(packed, "expert", split_axis=0, concat_axis=0, tiled=True)
    rows = received.reshape(-1, feature_count)
    hidden = hidden_quarter(rows, gate_up)
    other_hidden = hidden_quarter(rows, other_gate_up)
    halves = jnp.dot(hidden, down_matrix, preferred_element_type=jnp.float32)
    halves = halves + jnp.dot(other_hidden, other_down, preferred_element_type=jnp.float32)
    halves = halves.reshape(held_count, 2, CAP, feature_count)
    other_half = along_dp(halves[:, 1].astype(jnp.bfloat16), False)
    rounded = (halves[:, 0] + other_half.astype(jnp.float32)).astype(jnp.bfloat16)
    returned = lax.all_to_all(rounded, "expert", split_axis=0, concat_axis=0, tiled=True)
    expert_sums = returned.astype(jnp.float32)
    shares = slot_table.astype(jnp.float32) * coefficient[..., None]
    mixture = jnp.einsum(
        "tec,ecd->td", shares, expert_sums, precision=lax.Precision.HIGHEST
    ).astype(jnp.bfloat16)
    return from_behind(mixture[None], "section", 1)


def solution(mesh):
    in_specs = (
        P("section", ("dp", "expert"), None),
        P("section", None),
        P("section", ("dp", "expert"), None),
        P("section", ("dp", "expert"), None),
        P("section", "expert", None, None, "dp"),
        P("section", "expert", "dp", None),
    )
    out_specs = P("section", ("dp", "expert"), None)
    return jax.shard_map(shards, mesh=mesh, in_specs=in_specs, out_specs=out_specs, check_vma=False)
```

```python
import functools

import jax
import jax.numpy as jnp
import numpy as np
from jax import lax
from jax.experimental import pallas as pl
from jax.experimental.pallas import tpu as pltpu
from jax.sharding import PartitionSpec as P

MESH = pl.DeviceIdType.MESH
CAP = 12
EPSILON = 1e-06
NZ = 8
NX = 4
NF = 4
SLAB = CAP * NF
F32 = jnp.float32
BF16 = jnp.bfloat16


def mm(a, b):
    return jnp.dot(a, b, preferred_element_type=F32)


def kernel(
    stream, gain, probs, ids, gu_hbm, dn_hbm, unpack, repack, out,
    raw, code, coef, grid, stacked, psend, drec, gu, dn, mine, ysend, yrecv, zsend, rec,
    shares, osend, hop,
    raw_ss, raw_rs, d_ss, d_rs, w_ss, w_rs, l_sem, y_ss, y_rs, s_ss, s_rs, h_ss, h_rs,
):
    tokens, features = stream.shape
    width = features // NF
    held = NZ * NX
    section, group, me = lax.axis_index("section"), lax.axis_index("dp"), lax.axis_index("expert")
    z, x = me // NX, me % NX
    core = section % 2
    beside = group + 1 - 2 * (group % 2)
    across = 3 - group
    row_mate = core * beside + (1 - core) * across
    weight_mate = (1 - core) * beside + core * across
    ahead, behind = (section + 1) % 4, (section + 3) % 4

    def peer(step):
        turn = step // NX
        zs = (z + 4 + (1 - 2 * (turn % 2)) * ((turn + 1) // 2)) % NZ
        return zs, zs * NX + (x + step % NX) % NX

    last = held - NX

    barrier = pltpu.get_barrier_semaphore()
    pl.semaphore_signal(barrier, inc=1, device_id={"dp": row_mate}, device_id_type=MESH)
    pl.semaphore_signal(barrier, inc=1, device_id={"dp": weight_mate}, device_id_type=MESH)
    pl.semaphore_signal(barrier, inc=1, device_id={"section": behind}, device_id_type=MESH)

    def greet(j, carry):
        pl.semaphore_signal(
            barrier, inc=1, device_id={"expert": (me + j) % held}, device_id_type=MESH
        )
        return carry

    lax.fori_loop(1, held, greet, 0)
    own_gu = pltpu.make_async_copy(gu_hbm, gu.at[0], l_sem.at[0])
    own_gu.start()
    own_dn = pltpu.make_async_copy(dn_hbm, dn.at[0], l_sem.at[1])
    own_dn.start()

    wide = stream[...].astype(F32)
    inverse = lax.rsqrt(jnp.mean(wide * wide, axis=-1, keepdims=True) + EPSILON)
    raw[0] = (wide * inverse * gain[...].astype(F32)).astype(BF16)

    expert_iota = lax.broadcasted_iota(jnp.int32, (held, tokens), 0)
    weights = probs[...] / jnp.sum(probs[...], axis=0, keepdims=True)
    chosen = jnp.zeros((held, tokens), F32)
    total = jnp.zeros((held, tokens), F32)
    for k in range(ids.shape[0]):
        match = ids[k : k + 1, :] == expert_iota
        chosen = chosen + jnp.where(match, 1.0, 0.0)
        total = total + jnp.where(match, weights[k : k + 1, :], 0.0)
    earlier = lax.broadcasted_iota(jnp.int32, (tokens, tokens), 0) < lax.broadcasted_iota(
        jnp.int32, (tokens, tokens), 1
    )
    position = mm(chosen.astype(BF16), jnp.where(earlier, 1.0, 0.0).astype(BF16))
    code[0] = jnp.where(chosen > 0.5, position, -1.0)
    coef[...] = total

    pl.semaphore_wait(barrier, held - 1 + 3)

    def to_mate(src, dst, k):
        return pltpu.make_async_remote_copy(
            src_ref=src, dst_ref=dst, send_sem=raw_ss.at[k], recv_sem=raw_rs.at[k],
            device_id={"dp": row_mate}, device_id_type=MESH,
        )

    raw_copy = to_mate(raw.at[0], raw.at[1], 0)
    code_copy = to_mate(code.at[0], code.at[1], 1)
    code_copy.start()
    raw_copy.start()

    row_iota = lax.broadcasted_iota(jnp.int32, (SLAB, tokens), 0)
    row_block = jnp.where(row_iota >= CAP, 1, 0)
    for f in range(2, NF):
        row_block = row_block + jnp.where(row_iota >= CAP * f, 1, 0)
    row_slot = (row_iota - CAP * row_block).astype(F32)

    def dispatch_copy(d, step):
        _, other = peer(step)
        return pltpu.make_async_remote_copy(
            src_ref=psend.at[d, other], dst_ref=drec.at[me, d],
            send_sem=d_ss.at[d, step], recv_sem=d_rs.at[d, me],
            device_id={"expert": other}, device_id_type=MESH,
        )

    def dispatch(d):
        def fill(e, carry):
            hit = code[d, pl.ds(e, 1), :] == row_slot
            for f in range(NF):
                grid[pl.ds(pl.multiple_of(e * SLAB, SLAB), SLAB), f * tokens : (f + 1) * tokens] = (
                    jnp.where(hit, jnp.where(row_block == f, 1.0, 0.0), 0.0).astype(BF16)
                )
            return carry

        lax.fori_loop(0, held, fill, 0)
        for f in range(NF):
            stacked[f * tokens : (f + 1) * tokens, :] = raw[d, :, f * width : (f + 1) * width]

        def pack(j, carry):
            rows = pl.ds(pl.multiple_of(j * 8 * SLAB, 8 * SLAB), 8 * SLAB)
            slabs = mm(grid[rows, :], stacked[...]).astype(BF16)
            psend[d, pl.ds(j * 8, 8)] = slabs.reshape(8, SLAB, width)
            return carry

        lax.fori_loop(0, held // 8, pack, 0)

        def send(step, carry):
            dispatch_copy(d, step).start()
            return carry

        lax.fori_loop(0, last, send, 0)
        lax.fori_loop(last + 1, held, send, 0)
        drec[me, d] = psend[d, me]

    dispatch(0)
    raw_copy.wait()
    code_copy.wait()

    def to_weight_mate(src, dst, k):
        return pltpu.make_async_remote_copy(
            src_ref=src, dst_ref=dst, send_sem=w_ss.at[k], recv_sem=w_rs.at[k],
            device_id={"dp": weight_mate}, device_id_type=MESH,
        )

    gu_copy = to_weight_mate(gu_hbm, gu.at[1], 0)
    dn_copy = to_weight_mate(dn_hbm, dn.at[1], 1)
    gu_copy.start()
    dn_copy.start()
    dispatch(1)

    def share(e, carry):
        hit = code[0, pl.ds(e, 1), :] == row_slot
        value = coef[pl.ds(e, 1), :]
        high = value.astype(BF16).astype(F32)
        low = value - high
        rows = pl.ds(pl.multiple_of(e * SLAB, SLAB), SLAB)
        for f in range(NF):
            here = jnp.where(hit, jnp.where(row_block == f, 1.0, 0.0), 0.0)
            base = 2 * f * tokens
            shares[rows, base : base + tokens] = (here * high).astype(BF16)
            shares[rows, base + tokens : base + 2 * tokens] = (here * low).astype(BF16)
        return carry

    lax.fori_loop(0, held, share, 0)

    own_gu.wait()
    own_dn.wait()
    gu_copy.wait()
    dn_copy.wait()

    def y_copy(turn):
        return pltpu.make_async_remote_copy(
            src_ref=ysend.at[turn], dst_ref=yrecv.at[turn],
            send_sem=y_ss.at[turn], recv_sem=y_rs.at[turn],
            device_id={"dp": row_mate}, device_id_type=MESH,
        )

    def arrived(other):
        for d in range(2):
            pltpu.make_async_remote_copy(
                src_ref=psend.at[d, other], dst_ref=drec.at[other, d],
                send_sem=d_ss.at[d, 0], recv_sem=d_rs.at[d, other],
                device_id={"expert": other}, device_id_type=MESH,
            ).wait_recv()

    per_z = NX * CAP

    def expert_block(turn, own):
        zs, _ = peer(turn * NX)
        for k in range(1 if own else 0, NX):
            arrived(peer(turn * NX + k)[1])
        block = drec[pl.ds(zs * NX, NX)].reshape(NX * 2 * SLAB, width)
        rows = mm(unpack[...], block).astype(BF16)
        result = jnp.zeros((2 * per_z, features), F32)
        for half in range(2):
            gate = jnp.zeros((2 * per_z, gu.shape[3]), F32)
            up = jnp.zeros((2 * per_z, gu.shape[3]), F32)
            for f in range(NF):
                part = rows[f * 2 * per_z : (f + 1) * 2 * per_z, :]
                gate = gate + mm(part, gu[half, 0, f * width : (f + 1) * width, :])
                up = up + mm(part, gu[half, 1, f * width : (f + 1) * width, :])
            hidden = (gate / (1.0 + jnp.exp(-gate)) * up).astype(BF16)
            result = result + mm(hidden, dn[half])
        mine[turn] = result[:per_z]
        ysend[turn] = result[per_z:].astype(BF16)
        y_copy(turn).start()

    def back_copy(step):
        _, other = peer(step)
        return pltpu.make_async_remote_copy(
            src_ref=zsend.at[step // NX, other % NX], dst_ref=rec.at[me],
            send_sem=s_ss.at[step], recv_sem=s_rs.at[me],
            device_id={"expert": other}, device_id_type=MESH,
        )

    def give_back(turn, own):
        y_copy(turn).wait_recv()
        summed = (mine[turn] + yrecv[turn].astype(F32)).astype(BF16)
        tall = jnp.concatenate(
            [summed[:, f * width : (f + 1) * width] for f in range(NF)], axis=0
        )
        zsend[turn] = mm(repack[...], tall).astype(BF16).reshape(NX, SLAB, width)
        for k in range(1 if own else 0, NX):
            back_copy(turn * NX + k).start()
        if own:
            rec[me] = zsend[turn, x]

    expert_block(0, False)
    expert_block(1, False)

    def steady(turn, carry):
        expert_block(turn, False)
        give_back(turn - 2, False)
        return carry

    lax.fori_loop(2, NZ - 1, steady, 0)
    expert_block(NZ - 1, True)
    give_back(NZ - 3, False)
    give_back(NZ - 2, False)
    give_back(NZ - 1, True)

    def returned(j, carry):
        other = (me + j) % held
        pltpu.make_async_remote_copy(
            src_ref=zsend.at[0, 0], dst_ref=rec.at[other],
            send_sem=s_ss.at[0], recv_sem=s_rs.at[other],
            device_id={"expert": other}, device_id_type=MESH,
        ).wait_recv()
        return carry

    lax.fori_loop(1, held, returned, 0)

    def hop_copy(f):
        return pltpu.make_async_remote_copy(
            src_ref=osend.at[f], dst_ref=hop.at[f], send_sem=h_ss.at[f], recv_sem=h_rs.at[f],
            device_id={"section": ahead}, device_id_type=MESH,
        )

    everything = rec[...].reshape(held * SLAB, width)
    for f in range(NF):
        both = lax.dot_general(
            shares[:, 2 * f * tokens : 2 * (f + 1) * tokens], everything,
            (((0,), (0,)), ((), ())), preferred_element_type=F32,
        )
        osend[f] = (both[:tokens] + both[tokens:]).astype(BF16)
        hop_copy(f).start()

    def left(step, carry):
        for d in range(2):
            dispatch_copy(d, step).wait_send()
        back_copy(step).wait_send()
        return carry

    lax.fori_loop(0, last, left, 0)
    lax.fori_loop(last + 1, held, left, 0)

    def left_along_y(turn, carry):
        y_copy(turn).wait_send()
        return carry

    lax.fori_loop(0, NZ, left_along_y, 0)
    for f in range(NF):
        hop_copy(f).wait()
        out[:, f * width : (f + 1) * width] = hop[f]


def moves():
    per_z = NX * CAP
    unpack = np.zeros((NF * 2 * per_z, NX * 2 * SLAB), np.float32)
    repack = np.zeros((NX * SLAB, NX * SLAB), np.float32)
    for f in range(NF):
        for xs in range(NX):
            for c in range(CAP):
                for d in range(2):
                    unpack[((f * 2 + d) * NX + xs) * CAP + c, ((xs * 2 + d) * NF + f) * CAP + c] = 1
                repack[(xs * NF + f) * CAP + c, (f * NX + xs) * CAP + c] = 1
    return jnp.asarray(unpack, BF16), jnp.asarray(repack, BF16)


def shards(stream, norm_gain, gate_probs, expert_ids, gate_up_weight, down_weight):
    tokens, features = stream.shape[1:]
    held = NZ * NX
    width = features // NF
    units = gate_up_weight.shape[4]
    unpack, repack = moves()
    vmem = pl.BlockSpec(memory_space=pltpu.VMEM)
    anywhere = pl.BlockSpec(memory_space=pl.ANY)
    dma = pltpu.SemaphoreType.DMA
    result = pl.pallas_call(
        kernel,
        out_shape=jax.ShapeDtypeStruct((tokens, features), BF16),
        in_specs=[vmem, vmem, vmem, vmem, anywhere, anywhere, vmem, vmem],
        out_specs=vmem,
        scratch_shapes=[
            pltpu.VMEM((2, tokens, features), BF16),
            pltpu.VMEM((2, held, tokens), F32),
            pltpu.VMEM((held, tokens), F32),
            pltpu.VMEM((held * SLAB, NF * tokens), BF16),
            pltpu.VMEM((NF * tokens, width), BF16),
            pltpu.VMEM((2, held, SLAB, width), BF16),
            pltpu.VMEM((held, 2, SLAB, width), BF16),
            pltpu.VMEM((2, 2, features, units), BF16),
            pltpu.VMEM((2, units, features), BF16),
            pltpu.VMEM((NZ, NX * CAP, features), F32),
            pltpu.VMEM((NZ, NX * CAP, features), BF16),
            pltpu.VMEM((NZ, NX * CAP, features), BF16),
            pltpu.VMEM((NZ, NX, SLAB, width), BF16),
            pltpu.VMEM((held, SLAB, width), BF16),
            pltpu.VMEM((held * SLAB, 2 * NF * tokens), BF16),
            pltpu.VMEM((NF, tokens, width), BF16),
            pltpu.VMEM((NF, tokens, width), BF16),
            dma((2,)), dma((2,)), dma((2, held)), dma((2, held)), dma((2,)), dma((2,)),
            dma((2,)), dma((NZ,)), dma((NZ,)), dma((held,)), dma((held,)),
            dma((NF,)), dma((NF,)),
        ],
        compiler_params=pltpu.CompilerParams(
            collective_id=0, has_side_effects=True, vmem_limit_bytes=56 << 20
        ),
        name="routed",
    )(
        stream[0], norm_gain, gate_probs[0].T, expert_ids[0].T,
        gate_up_weight[0, 0], down_weight[0, 0], unpack, repack,
    )
    return result[None]


def solution(mesh):
    in_specs = (
        P("section", ("dp", "expert"), None),
        P("section", None),
        P("section", ("dp", "expert"), None),
        P("section", ("dp", "expert"), None),
        P("section", "expert", None, None, "dp"),
        P("section", "expert", "dp", None),
    )
    out_specs = P("section", ("dp", "expert"), None)
    return jax.shard_map(shards, mesh=mesh, in_specs=in_specs, out_specs=out_specs, check_vma=False)
```

```python
import functools

import jax
import jax.numpy as jnp
import numpy as np
from jax import lax
from jax.experimental import pallas as pl
from jax.experimental.pallas import tpu as pltpu
from jax.sharding import PartitionSpec as P

MESH = pl.DeviceIdType.MESH
CAP = 12
EPSILON = 1e-06
NZ = 8
NX = 4
NF = 4
SLAB = CAP * NF
F32 = jnp.float32
BF16 = jnp.bfloat16


def mm(a, b):
    return jnp.dot(a, b, preferred_element_type=F32)


def kernel(
    stream, gain, probs, ids, gu_hbm, dn_hbm, unpack, repack, out,
    raw, code, coef, grid, stacked, psend, drec, gu, dn, rows, mine, hid, ysend, yrecv, zsend, rec,
    shares, osend, hop,
    raw_ss, raw_rs, d_ss, d_rs, w_ss, w_rs, l_sem, y_ss, y_rs, s_ss, s_rs, h_ss, h_rs, plane_sem,
):
    tokens, features = stream.shape
    width = features // NF
    held = NZ * NX
    section, group, me = lax.axis_index("section"), lax.axis_index("dp"), lax.axis_index("expert")
    z, x = me // NX, me % NX
    core = section % 2
    beside = group + 1 - 2 * (group % 2)
    across = 3 - group
    row_mate = core * beside + (1 - core) * across
    weight_mate = (1 - core) * beside + core * across
    ahead, behind = (section + 1) % 4, (section + 3) % 4

    def peer(step):
        turn = step // NX
        zs = (z + 4 + (1 - 2 * (turn % 2)) * ((turn + 1) // 2)) % NZ
        return zs, zs * NX + (x + step % NX) % NX

    last = held - NX

    barrier = pltpu.get_barrier_semaphore()
    pl.semaphore_signal(barrier, inc=1, device_id={"dp": row_mate}, device_id_type=MESH)
    pl.semaphore_signal(barrier, inc=1, device_id={"dp": weight_mate}, device_id_type=MESH)
    pl.semaphore_signal(barrier, inc=1, device_id={"section": behind}, device_id_type=MESH)

    along_x = [z * NX + (x + k) % NX for k in range(1, NX)]
    along_z = [(z + k) % NZ * NX + x for k in range(1, NZ)]
    for other in along_x + along_z:
        pl.semaphore_signal(barrier, inc=1, device_id={"expert": other}, device_id_type=MESH)
    own_gu = pltpu.make_async_copy(gu_hbm, gu.at[0], l_sem.at[0])
    own_gu.start()
    own_dn = pltpu.make_async_copy(dn_hbm, dn.at[0], l_sem.at[1])
    own_dn.start()

    wide = stream[...].astype(F32)
    inverse = lax.rsqrt(jnp.mean(wide * wide, axis=-1, keepdims=True) + EPSILON)
    raw[0] = (wide * inverse * gain[...].astype(F32)).astype(BF16)

    expert_iota = lax.broadcasted_iota(jnp.int32, (held, tokens), 0)
    weights = probs[...] / jnp.sum(probs[...], axis=0, keepdims=True)
    chosen = jnp.zeros((held, tokens), F32)
    total = jnp.zeros((held, tokens), F32)
    for k in range(ids.shape[0]):
        match = ids[k : k + 1, :] == expert_iota
        chosen = chosen + jnp.where(match, 1.0, 0.0)
        total = total + jnp.where(match, weights[k : k + 1, :], 0.0)
    earlier = lax.broadcasted_iota(jnp.int32, (tokens, tokens), 0) < lax.broadcasted_iota(
        jnp.int32, (tokens, tokens), 1
    )
    position = mm(chosen.astype(BF16), jnp.where(earlier, 1.0, 0.0).astype(BF16))
    code[0] = jnp.where(chosen > 0.5, position, -1.0)
    coef[...] = total

    pl.semaphore_wait(barrier, len(along_x + along_z) + 3)

    def to_mate(src, dst, k):
        return pltpu.make_async_remote_copy(
            src_ref=src, dst_ref=dst, send_sem=raw_ss.at[k], recv_sem=raw_rs.at[k],
            device_id={"dp": row_mate}, device_id_type=MESH,
        )

    raw_copy = to_mate(raw.at[0], raw.at[1], 0)
    code_copy = to_mate(code.at[0], code.at[1], 1)
    code_copy.start()
    raw_copy.start()

    def to_weight_mate(src, dst, k):
        return pltpu.make_async_remote_copy(
            src_ref=src, dst_ref=dst, send_sem=w_ss.at[k], recv_sem=w_rs.at[k],
            device_id={"dp": weight_mate}, device_id_type=MESH,
        )

    weight_copies = [
        to_weight_mate(gu.at[0, 0], gu.at[1, 0], 0),
        to_weight_mate(gu.at[0, 1], gu.at[1, 1], 1),
        to_weight_mate(dn.at[0], dn.at[1], 2),
    ]
    own_gu.wait()
    own_dn.wait()
    weight_copies[0].start()
    for other in along_x:
        pl.semaphore_signal(plane_sem, inc=1, device_id={"expert": other}, device_id_type=MESH)

    row_iota = lax.broadcasted_iota(jnp.int32, (SLAB, tokens), 0)
    row_block = jnp.where(row_iota >= CAP, 1, 0)
    for f in range(2, NF):
        row_block = row_block + jnp.where(row_iota >= CAP * f, 1, 0)
    row_slot = (row_iota - CAP * row_block).astype(F32)

    def dispatch_copy(d, step):
        _, other = peer(step)
        return pltpu.make_async_remote_copy(
            src_ref=psend.at[d, other], dst_ref=drec.at[me, d],
            send_sem=d_ss.at[d, step], recv_sem=d_rs.at[d, me],
            device_id={"expert": other}, device_id_type=MESH,
        )

    def dispatch(d):
        def fill(e, carry):
            hit = code[d, pl.ds(e, 1), :] == row_slot
            for f in range(NF):
                grid[pl.ds(pl.multiple_of(e * SLAB, SLAB), SLAB), f * tokens : (f + 1) * tokens] = (
                    jnp.where(hit, jnp.where(row_block == f, 1.0, 0.0), 0.0).astype(BF16)
                )
            return carry

        lax.fori_loop(0, held, fill, 0)
        for f in range(NF):
            stacked[f * tokens : (f + 1) * tokens, :] = raw[d, :, f * width : (f + 1) * width]

        def pack(j, carry):
            part = pl.ds(pl.multiple_of(j * 8 * SLAB, 8 * SLAB), 8 * SLAB)
            slabs = mm(grid[part, :], stacked[...]).astype(BF16)
            psend[d, pl.ds(j * 8, 8)] = slabs.reshape(8, SLAB, width)
            return carry

        lax.fori_loop(0, held // 8, pack, 0)

        if d == 0:
            pl.semaphore_wait(plane_sem, len(along_x))

        def send(step, carry):
            dispatch_copy(d, step).start()
            return carry

        lax.fori_loop(0, last, send, 0)
        lax.fori_loop(last + 1, held, send, 0)
        drec[me, d] = psend[d, me]

    dispatch(0)
    raw_copy.wait()
    code_copy.wait()

    weight_copies[1].start()
    weight_copies[2].start()
    dispatch(1)

    def share(e, carry):
        hit = code[0, pl.ds(e, 1), :] == row_slot
        value = coef[pl.ds(e, 1), :]
        high = value.astype(BF16).astype(F32)
        low = value - high
        part = pl.ds(pl.multiple_of(e * SLAB, SLAB), SLAB)
        for f in range(NF):
            here = jnp.where(hit, jnp.where(row_block == f, 1.0, 0.0), 0.0)
            base = 2 * f * tokens
            shares[part, base : base + tokens] = (here * high).astype(BF16)
            shares[part, base + tokens : base + 2 * tokens] = (here * low).astype(BF16)
        return carry

    lax.fori_loop(0, held, share, 0)


    def y_copy(turn):
        return pltpu.make_async_remote_copy(
            src_ref=ysend.at[turn], dst_ref=yrecv.at[turn],
            send_sem=y_ss.at[turn], recv_sem=y_rs.at[turn],
            device_id={"dp": row_mate}, device_id_type=MESH,
        )

    per_z = NX * CAP

    def gather(d):
        def arrived(j, carry):
            other = (me + j) % held
            pltpu.make_async_remote_copy(
                src_ref=psend.at[d, other], dst_ref=drec.at[other, d],
                send_sem=d_ss.at[d, 0], recv_sem=d_rs.at[d, other],
                device_id={"expert": other}, device_id_type=MESH,
            ).wait_recv()
            return carry

        lax.fori_loop(1, held, arrived, 0)

        def sort(zs, carry):
            block = drec[pl.ds(zs * NX, NX), d].reshape(NX * SLAB, width)
            sorted_rows = mm(unpack[...], block).astype(BF16)
            for f in range(NF):
                rows[d, f, pl.ds(pl.multiple_of(zs * per_z, per_z), per_z), :] = sorted_rows[
                    f * per_z : (f + 1) * per_z, :
                ]
            return carry

        lax.fori_loop(0, NZ, sort, 0)

    def hide(d, half):
        gate = jnp.zeros((NZ * per_z, gu.shape[3]), F32)
        up = jnp.zeros((NZ * per_z, gu.shape[3]), F32)
        for f in range(NF):
            part = rows[d, f]
            gate = gate + mm(part, gu[half, 0, f * width : (f + 1) * width, :])
            up = up + mm(part, gu[half, 1, f * width : (f + 1) * width, :])
        return (gate / (1.0 + jnp.exp(-gate)) * up).astype(BF16)

    def block_of(turn):
        zs, _ = peer(turn * NX)
        return pl.ds(pl.multiple_of(zs * per_z, per_z), per_z)

    def lend(turn, carry):
        here = block_of(turn)
        ysend[turn] = (mine[1, here, :] + mm(hid[here, :], dn[1])).astype(BF16)
        y_copy(turn).start()
        return carry

    def back_copy(step):
        _, other = peer(step)
        return pltpu.make_async_remote_copy(
            src_ref=zsend.at[step // NX, other % NX], dst_ref=rec.at[me],
            send_sem=s_ss.at[step], recv_sem=s_rs.at[me],
            device_id={"expert": other}, device_id_type=MESH,
        )

    def give_back(turn, own):
        y_copy(turn).wait_recv()
        summed = (mine[0, block_of(turn), :] + yrecv[turn].astype(F32)).astype(BF16)
        tall = jnp.concatenate(
            [summed[:, f * width : (f + 1) * width] for f in range(NF)], axis=0
        )
        zsend[turn] = mm(repack[...], tall).astype(BF16).reshape(NX, SLAB, width)
        for k in range(1 if own else 0, NX):
            back_copy(turn * NX + k).start()
        if own:
            rec[me] = zsend[turn, x]

    for d in range(2):
        gather(d)
        mine[d] = mm(hide(d, 0), dn[0])
    weight_copies[0].wait()
    weight_copies[1].wait()
    hid[...] = hide(1, 1)
    weight_copies[2].wait()
    lax.fori_loop(0, NZ, lend, 0)
    mine[0] = mine[0] + mm(hide(0, 1), dn[1])

    def steady(turn, carry):
        give_back(turn, False)
        return carry

    lax.fori_loop(0, NZ - 1, steady, 0)
    give_back(NZ - 1, True)

    def returned(j, carry):
        other = (me + j) % held
        pltpu.make_async_remote_copy(
            src_ref=zsend.at[0, 0], dst_ref=rec.at[other],
            send_sem=s_ss.at[0], recv_sem=s_rs.at[other],
            device_id={"expert": other}, device_id_type=MESH,
        ).wait_recv()
        return carry

    lax.fori_loop(1, held, returned, 0)

    def hop_copy(f):
        return pltpu.make_async_remote_copy(
            src_ref=osend.at[f], dst_ref=hop.at[f], send_sem=h_ss.at[f], recv_sem=h_rs.at[f],
            device_id={"section": ahead}, device_id_type=MESH,
        )

    everything = rec[...].reshape(held * SLAB, width)
    for f in range(NF):
        both = lax.dot_general(
            shares[:, 2 * f * tokens : 2 * (f + 1) * tokens], everything,
            (((0,), (0,)), ((), ())), preferred_element_type=F32,
        )
        osend[f] = (both[:tokens] + both[tokens:]).astype(BF16)
        hop_copy(f).start()

    def left(step, carry):
        for d in range(2):
            dispatch_copy(d, step).wait_send()
        back_copy(step).wait_send()
        return carry

    lax.fori_loop(0, last, left, 0)
    lax.fori_loop(last + 1, held, left, 0)

    def left_along_y(turn, carry):
        y_copy(turn).wait_send()
        return carry

    lax.fori_loop(0, NZ, left_along_y, 0)
    for f in range(NF):
        hop_copy(f).wait()
        out[:, f * width : (f + 1) * width] = hop[f]


def moves():
    repack = np.zeros((NX * SLAB, NX * SLAB), np.float32)
    for f in range(NF):
        for xs in range(NX):
            for c in range(CAP):
                repack[(xs * NF + f) * CAP + c, (f * NX + xs) * CAP + c] = 1
    unpack = repack.T
    return jnp.asarray(unpack, BF16), jnp.asarray(repack, BF16)


def shards(stream, norm_gain, gate_probs, expert_ids, gate_up_weight, down_weight):
    tokens, features = stream.shape[1:]
    held = NZ * NX
    width = features // NF
    units = gate_up_weight.shape[4]
    unpack, repack = moves()
    vmem = pl.BlockSpec(memory_space=pltpu.VMEM)
    anywhere = pl.BlockSpec(memory_space=pl.ANY)
    dma = pltpu.SemaphoreType.DMA
    result = pl.pallas_call(
        kernel,
        out_shape=jax.ShapeDtypeStruct((tokens, features), BF16),
        in_specs=[vmem, vmem, vmem, vmem, anywhere, anywhere, vmem, vmem],
        out_specs=vmem,
        scratch_shapes=[
            pltpu.VMEM((2, tokens, features), BF16),
            pltpu.VMEM((2, held, tokens), F32),
            pltpu.VMEM((held, tokens), F32),
            pltpu.VMEM((held * SLAB, NF * tokens), BF16),
            pltpu.VMEM((NF * tokens, width), BF16),
            pltpu.VMEM((2, held, SLAB, width), BF16),
            pltpu.VMEM((held, 2, SLAB, width), BF16),
            pltpu.VMEM((2, 2, features, units), BF16),
            pltpu.VMEM((2, units, features), BF16),
            pltpu.VMEM((2, NF, held * CAP, width), BF16),
            pltpu.VMEM((2, held * CAP, features), F32),
            pltpu.VMEM((held * CAP, units), BF16),
            pltpu.VMEM((NZ, NX * CAP, features), BF16),
            pltpu.VMEM((NZ, NX * CAP, features), BF16),
            pltpu.VMEM((NZ, NX, SLAB, width), BF16),
            pltpu.VMEM((held, SLAB, width), BF16),
            pltpu.VMEM((held * SLAB, 2 * NF * tokens), BF16),
            pltpu.VMEM((NF, tokens, width), BF16),
            pltpu.VMEM((NF, tokens, width), BF16),
            dma((2,)), dma((2,)), dma((2, held)), dma((2, held)), dma((3,)), dma((3,)),
            dma((2,)), dma((NZ,)), dma((NZ,)), dma((held,)), dma((held,)),
            dma((NF,)), dma((NF,)), pltpu.SemaphoreType.REGULAR,
        ],
        compiler_params=pltpu.CompilerParams(
            collective_id=0, has_side_effects=True, vmem_limit_bytes=56 << 20
        ),
        name="routed",
    )(
        stream[0], norm_gain, gate_probs[0].T, expert_ids[0].T,
        gate_up_weight[0, 0], down_weight[0, 0], unpack, repack,
    )
    return result[None]


def solution(mesh):
    in_specs = (
        P("section", ("dp", "expert"), None),
        P("section", None),
        P("section", ("dp", "expert"), None),
        P("section", ("dp", "expert"), None),
        P("section", "expert", None, None, "dp"),
        P("section", "expert", "dp", None),
    )
    out_specs = P("section", ("dp", "expert"), None)
    return jax.shard_map(shards, mesh=mesh, in_specs=in_specs, out_specs=out_specs, check_vma=False)
```
